32 devices in a mesh: dp: 8 (over z, y), tensor: 4 (over x, core).
Axes of the slice: x: 2, y: 2, z: 4, core: 2. Of those that a mesh axis runs over, the one named last changes fastest.
Arguments:
- inputs: bfloat16 [1024, 3200], P('dp'), may hold values from -6 to 6
- norm_gain: float32 [3200], replicated, may hold values from 0.25 to 1.75
- fc1_weight: bfloat16 [3200, 8192], P(None, 'tensor'), may hold values from -0.109375 to 0.109375
- fc1_bias: float32 [8192], P('tensor'), may hold values from -4 to 4
- grad_act: bfloat16 [1024, 8192], P('dp', 'tensor'), may hold values from -6 to 6
- grad_res: bfloat16 [1024, 3200], P(('dp', 'tensor')), may hold values from -6 to 6
Outputs:
- grad_inputs: bfloat16 [1024, 3200], P(('dp', 'tensor'))
- grad_weight: float32 [3200, 8192], P('dp', 'tensor')
- grad_bias: float32 [8192], P('tensor')
- grad_gain: float32 [3200], replicated
The draws below stay inside these ranges and needn't reach their ends.
All inputs are finite; a program needn't handle non-finite values.
Results may differ from the reference program's by a relative error of at most 0.008.
Values may be sent and summed in bfloat16 or wider, within the bound.
No kernel may reach another device: no remote copies, remote signals or barrier semaphores. Data moves between devices by JAX's collectives and lax.ppermute only.
A program may use at most 192 MiB of HBM per device.

```python
import jax
import jax.numpy as jnp
from jax import lax

D = 3200
FF = 8192
TOKENS = 1024
N_TENSOR = 4


def strengthened(array, stream_key, source, target, shards_of, factor):
    owner, partner = [(jnp.arange(array.shape[axis_at]) // (array.shape[axis_at] // shards_of)).reshape([-1 if axis == axis_at else 1 for axis in range(array.ndim)]) for axis_at in (source, target)]
    chosen = jax.random.permutation(stream_key, shards_of)[partner]
    strong = (owner == chosen) | (owner == (partner + shards_of // 2) % shards_of)
    return jnp.where(strong, factor * array, array)


def level_of(rng, dims, shards, smallest, high):
    loudness = 1.0
    for axis_at, parts in shards:
        steps = jax.random.uniform(jax.random.fold_in(jax.random.fold_in(rng, 6), axis_at), (parts,), jnp.float32, smallest / len(shards), high / len(shards))
        loudness = loudness * jnp.repeat(jnp.exp(steps), dims[axis_at] // parts).reshape((-1,) + (1,) * (len(dims) - 1 - axis_at))
    return loudness


def centred(rng, shape, spread, most, pieces=(), dtype=jnp.bfloat16):
    level = level_of(rng, shape, pieces, -0.22, 0.18) if pieces else 1.0
    array = jax.random.normal(rng, shape, jnp.float32) * spread * level
    return jnp.minimum(jnp.maximum(array, -most), most).astype(dtype)


def gaussian_with(key, shape, scale, most, split, heavy, kind=jnp.bfloat16):
    array = scale * jax.random.normal(key, shape, jnp.float32)
    if split:
        array = array * level_of(key, shape, split, -0.22, 0.18)
    return jnp.clip(strengthened(array, jax.random.fold_in(key, 3), *heavy), -most, most).astype(kind)


def setup_inputs(seed: int = 0) -> dict:
    arg_keys = jax.random.split(jax.random.key(seed), 7)
    inputs = gaussian_with(arg_keys[0], (TOKENS, D), 1.0, 6.0, ((0, 8),), (0, 1, 8, 2.0))
    norm_gain = jnp.clip(1.0 + 0.15 * jax.random.normal(arg_keys[1], (D,), jnp.float32), 0.25, 1.75)
    fc1_weight = centred(arg_keys[2], (D, FF), D ** -0.5, 0.109375, ((1, 4),))
    fc1_bias = centred(arg_keys[3], (FF,), 0.7, 4.0, ((0, 4),), jnp.float32)
    grad_act = centred(arg_keys[4], (TOKENS, FF), 1.0, 6.0, ((0, 8), (1, 4)))
    grad_res = centred(arg_keys[5], (TOKENS, D), 1.0, 6.0, ((0, 32),))
    return {"inputs": inputs, "norm_gain": norm_gain, "fc1_weight": fc1_weight, "fc1_bias": fc1_bias, "grad_act": grad_act, "grad_res": grad_res}


epsilon = 1e-06

def reference(inputs, norm_gain, fc1_weight, fc1_bias, grad_act, grad_res):
    values = inputs.astype(jnp.float32)
    inverse = lax.rsqrt(lax.optimization_barrier(jnp.mean(values * values, axis=-1, keepdims=True)) + epsilon)
    normalized = values * inverse
    normed = (normalized * norm_gain).astype(jnp.bfloat16)
    preact = jnp.dot(normed, fc1_weight, preferred_element_type=jnp.float32) + fc1_bias
    derivative = 0.5 * (1.0 + lax.erf(preact * 0.7071067811865476)) + preact * jnp.exp(-0.5 * preact * preact) * 0.3989422804014327
    grad_pre = (grad_act.astype(jnp.float32) * derivative).astype(jnp.bfloat16)
    grad_weight = jnp.dot(normed.T, grad_pre, preferred_element_type=jnp.float32)
    grad_bias = lax.optimization_barrier(jnp.sum(grad_pre.astype(jnp.float32), axis=0))
    shard_cols = FF // N_TENSOR
    dnormed = jnp.zeros((TOKENS, D), jnp.float32)
    for shard_index in range(N_TENSOR):
        block_grad = grad_pre[:, shard_index * shard_cols:(shard_index + 1) * shard_cols]
        block_weight = fc1_weight[:, shard_index * shard_cols:(shard_index + 1) * shard_cols]
        block_term = jnp.dot(block_grad, block_weight.T, preferred_element_type=jnp.float32).astype(jnp.bfloat16)
        block_term = lax.optimization_barrier(block_term)
        dnormed = dnormed + block_term.astype(jnp.float32)
    grad_gain = lax.optimization_barrier(jnp.sum(dnormed * normalized, axis=0))
    grad_hat = dnormed * norm_gain
    projection = lax.optimization_barrier(jnp.mean(grad_hat * normalized, axis=-1, keepdims=True))
    grad_inputs = (grad_res.astype(jnp.float32) + inverse * (grad_hat - normalized * projection)).astype(jnp.bfloat16)
    return (grad_inputs, grad_weight, grad_bias, grad_gain)
```

```python
import jax
import jax.numpy as jnp
from jax import lax
from jax.sharding import PartitionSpec as P

epsilon = 1e-06


def on_device(inputs, norm_gain, fc1_weight, fc1_bias, grad_act, grad_res):
    dp_size = lax.axis_size("dp")
    tensor_size = lax.axis_size("tensor")
    tokens, width = inputs.shape
    owner_rows = width // dp_size
    values = inputs.astype(jnp.float32)
    inverse = lax.rsqrt(jnp.mean(values * values, axis=-1, keepdims=True) + epsilon)
    normalized = values * inverse
    normed = (normalized * norm_gain).astype(jnp.bfloat16)
    blocks = normed.reshape(tokens, dp_size, owner_rows).transpose(1, 0, 2)
    owned_cols = lax.all_to_all(blocks, "dp", 0, 0, tiled=True).reshape(dp_size * tokens, owner_rows)
    preact = jnp.dot(normed, fc1_weight, preferred_element_type=jnp.float32) + fc1_bias
    derivative = (
        0.5 * (1.0 + lax.erf(preact * 0.7071067811865476))
        + preact * jnp.exp(-0.5 * preact * preact) * 0.3989422804014327
    )
    grad_pre = (grad_act.astype(jnp.float32) * derivative).astype(jnp.bfloat16)
    grad_pre_all = lax.all_gather(grad_pre, "dp", axis=0, tiled=True)
    back_term = lax.dot_general(
        grad_pre, fc1_weight, (((1,), (1,)), ((), ())), preferred_element_type=jnp.float32
    )
    dnormed = lax.psum_scatter(
        back_term.astype(jnp.bfloat16), "tensor", scatter_dimension=0, tiled=True
    ).astype(jnp.float32)
    grad_weight = lax.dot_general(
        owned_cols, grad_pre_all, (((0,), (0,)), ((), ())), preferred_element_type=jnp.float32
    )
    grad_bias = jnp.sum(grad_pre_all.astype(jnp.float32), axis=0)
    row_count = tokens // tensor_size
    row_start = lax.axis_index("tensor") * row_count
    normalized_rows = lax.dynamic_slice_in_dim(normalized, row_start, row_count, 0)
    inverse_rows = lax.dynamic_slice_in_dim(inverse, row_start, row_count, 0)
    gain_part = jnp.sum(dnormed * normalized_rows, axis=0)
    grad_hat = dnormed * norm_gain
    projection = jnp.mean(grad_hat * normalized_rows, axis=-1, keepdims=True)
    grad_inputs = (
        grad_res.astype(jnp.float32) + inverse_rows * (grad_hat - normalized_rows * projection)
    ).astype(jnp.bfloat16)
    grad_gain = lax.psum(gain_part, ("dp", "tensor"))
    return (grad_inputs, grad_weight, grad_bias, grad_gain)


def solution(mesh):
    in_specs = (
        P("dp", None),
        P(),
        P(None, "tensor"),
        P("tensor"),
        P("dp", "tensor"),
        P(("dp", "tensor"), None),
    )
    out_specs = (P(("dp", "tensor"), None), P("dp", "tensor"), P("tensor"), P())
    return jax.shard_map(
        on_device, mesh=mesh, in_specs=in_specs, out_specs=out_specs, check_vma=False
    )
```

```python
import functools

import jax
import jax.numpy as jnp
from jax import lax
from jax.experimental import pallas as pl
from jax.experimental.pallas import tpu as pltpu
from jax.sharding import PartitionSpec as P

epsilon = 1e-06
CHUNKS = 2
BLOCK = 256
TILE = 16
LANES = 128

VMEM_GRANT = 12 * 1024 * 1024


def gelu_slope(preact):
    return (
        0.5 * (1.0 + lax.erf(preact * 0.7071067811865476))
        + preact * jnp.exp(-0.5 * preact * preact) * 0.3989422804014327
    )


def plain(inputs, norm_gain, fc1_weight, fc1_bias, grad_act, grad_res):
    dp_size = lax.axis_size("dp")
    tensor_size = lax.axis_size("tensor")
    tokens, width = inputs.shape
    owner_rows = width // dp_size
    values = inputs.astype(jnp.float32)
    inverse = lax.rsqrt(jnp.mean(values * values, axis=-1, keepdims=True) + epsilon)
    normalized = values * inverse
    normed = (normalized * norm_gain).astype(jnp.bfloat16)
    blocks = normed.reshape(tokens, dp_size, owner_rows).transpose(1, 0, 2)
    owned_cols = lax.all_to_all(blocks, "dp", 0, 0, tiled=True).reshape(dp_size * tokens, owner_rows)
    preact = jnp.dot(normed, fc1_weight, preferred_element_type=jnp.float32) + fc1_bias
    grad_pre = (grad_act.astype(jnp.float32) * gelu_slope(preact)).astype(jnp.bfloat16)
    grad_pre_all = lax.all_gather(grad_pre, "dp", axis=0, tiled=True)
    back_term = lax.dot_general(
        grad_pre, fc1_weight, (((1,), (1,)), ((), ())), preferred_element_type=jnp.float32
    )
    dnormed = lax.psum_scatter(
        back_term.astype(jnp.bfloat16), "tensor", scatter_dimension=0, tiled=True
    ).astype(jnp.float32)
    grad_weight = lax.dot_general(
        owned_cols, grad_pre_all, (((0,), (0,)), ((), ())), preferred_element_type=jnp.float32
    )
    grad_bias = jnp.sum(grad_pre_all.astype(jnp.float32), axis=0)
    row_count = tokens // tensor_size
    row_start = lax.axis_index("tensor") * row_count
    normalized_rows = lax.dynamic_slice_in_dim(normalized, row_start, row_count, 0)
    inverse_rows = lax.dynamic_slice_in_dim(inverse, row_start, row_count, 0)
    gain_part = jnp.sum(dnormed * normalized_rows, axis=0)
    grad_hat = dnormed * norm_gain
    projection = jnp.mean(grad_hat * normalized_rows, axis=-1, keepdims=True)
    grad_inputs = (
        grad_res.astype(jnp.float32) + inverse_rows * (grad_hat - normalized_rows * projection)
    ).astype(jnp.bfloat16)
    grad_gain = lax.psum(gain_part, ("dp", "tensor"))
    return (grad_inputs, grad_weight, grad_bias, grad_gain)


SCALAR = pl.BlockSpec(memory_space=pltpu.SMEM)
GRANT = pltpu.CompilerParams(vmem_limit_bytes=VMEM_GRANT)
NEAR = pl.BlockSpec(memory_space=pltpu.VMEM)
FAR = pl.BlockSpec(memory_space=pltpu.HBM)


def forward_body(*refs, first, chunk, cols, stride):
    refs = list(refs)
    at_ref, dp_ref = refs.pop(0), refs.pop(0)
    if first:
        x_far, gain_far, bias_far, act_far, w_ref = (refs.pop(0) for _ in range(5))
        pre_ref, kept_ref, normed_ref, inverse_ref, x_ref, bias_ref, act_ref, gain_ref = (refs.pop(0) for _ in range(8))
    else:
        normed_ref, bias_ref, act_ref, w_ref = (refs.pop(0) for _ in range(4))
        pre_ref, kept_ref, stay_ref, send_ref, turned_ref = (refs.pop(0) for _ in range(5))
    sems = refs.pop(0)
    blocks = cols // BLOCK
    extra = []
    if first:
        pairs = [(x_far, x_ref), (gain_far, gain_ref), (act_far, act_ref), (bias_far, bias_ref)]
        extra = [pltpu.make_async_copy(far, near, sems.at[blocks + i]) for i, (far, near) in enumerate(pairs)]
        for copy in extra:
            copy.start()
    copies = [
        pltpu.make_async_copy(
            w_ref.at[:, pl.ds(chunk * cols + i * BLOCK, BLOCK)],
            kept_ref.at[:, pl.ds(i * BLOCK, BLOCK)],
            sems.at[i],
        )
        for i in range(blocks)
    ]
    for copy in copies:
        copy.start()
    if first:
        extra[0].wait()
        extra[1].wait()
        values = x_ref[...].astype(jnp.float32)
        inverse = lax.rsqrt(jnp.mean(values * values, axis=-1, keepdims=True) + epsilon)
        normed_ref[...] = (values * inverse * gain_ref[...][None, :]).astype(jnp.bfloat16)
        inverse_ref[...] = inverse
        extra[2].wait()
        extra[3].wait()
    else:
        kept_owners, span, _ = send_ref.shape
        width = normed_ref.shape[1]
        for i in range(width // LANES):
            turned_ref[i * LANES : (i + 1) * LANES, :] = normed_ref[:, i * LANES : (i + 1) * LANES].T
        low = dp_ref[0] % 2
        for half_owner in range(kept_owners):
            for target, bit in ((stay_ref, low), (send_ref, 1 - low)):
                owner = 2 * half_owner + bit
                start = pl.multiple_of(owner * (width // (2 * kept_owners)) + at_ref[0] * stride, TILE)
                target[half_owner] = turned_ref[pl.ds(start, span), :]
    for i in range(blocks):
        copies[i].wait()
        here = slice(i * BLOCK, (i + 1) * BLOCK)
        there = slice(chunk * cols + i * BLOCK, chunk * cols + (i + 1) * BLOCK)
        preact = jnp.dot(normed_ref[...], kept_ref[:, here], preferred_element_type=jnp.float32)
        preact = preact + bias_ref[there][None, :]
        slope = gelu_slope(preact)
        pre_ref[:, here] = (act_ref[:, there].astype(jnp.float32) * slope).astype(jnp.bfloat16)


def halve_body(dp_ref, stay_ref, got_ref, stay_out, send_out, *, bit, count):
    mine = (dp_ref[0] // 2**bit) % 2
    groups = 2**bit // 2
    rest = count // 2**bit
    for flipped, ref in enumerate((stay_ref, got_ref)):
        for source in range(groups):
            for owner in range(rest // 2):
                for out, wanted in ((stay_out, mine), (send_out, 1 - mine)):
                    out[(flipped * groups + source) * (rest // 2) + owner] = ref[source * rest + 2 * owner + wanted]


def join_body(a_ref, b_ref, out_ref):
    out_ref[0] = a_ref[...]
    out_ref[1] = b_ref[...]


def split_rows(row):
    high = row.astype(jnp.bfloat16)
    low = (row - high.astype(jnp.float32)).astype(jnp.bfloat16)
    which = lax.broadcasted_iota(jnp.int32, (TILE, row.shape[1]), 0)
    return jnp.where(which == 0, high.astype(jnp.float32), jnp.where(which == 1, low.astype(jnp.float32), 0.0)).astype(
        jnp.bfloat16
    )


def joined_row(rows):
    return jnp.sum(rows.astype(jnp.float32), axis=0, keepdims=True)


def backward_body(at_ref, *refs, chunks, feature):
    pre_refs = refs[:chunks]
    kept_refs = refs[chunks : 2 * chunks]
    x_ref, inverse_ref, stay_ref, send_ref, gain_ref, term_ref = refs[2 * chunks :]
    count = stay_ref.shape[0] // 2
    for j in range(x_ref.shape[1] // feature):
        here = slice(j * feature, (j + 1) * feature)
        term = None
        for pre_ref, kept_ref in zip(pre_refs, kept_refs):
            part = lax.dot_general(
                pre_ref[...],
                kept_ref[here, :],
                (((1,), (1,)), ((), ())),
                preferred_element_type=jnp.float32,
            )
            term = part if term is None else term + part
        term = term.astype(jnp.bfloat16)
        term_ref[:, here] = term
        normalized = x_ref[:, here].astype(jnp.float32) * inverse_ref[...]
        gain = jnp.sum(term.astype(jnp.float32) * normalized, axis=0, keepdims=True)
        gain_ref[:, here] = gain
        send_ref[2 * count :, here] = split_rows(gain)
    for slot in range(2):
        for ref, flip in ((stay_ref, 0), (send_ref, 1)):
            rows = pl.multiple_of((at_ref[0] ^ (flip + 2 * slot)) * count, TILE)
            ref[slot * count : (slot + 1) * count, :] = term_ref[pl.ds(rows, count), :]


def merge_body(stay_ref, got_ref, gain_ref, own_ref, send_ref, gain_out):
    count = own_ref.shape[0]
    own_ref[...] = stay_ref[:count, :].astype(jnp.float32) + got_ref[:count, :].astype(jnp.float32)
    far = stay_ref[count:, :].astype(jnp.float32) + got_ref[count : 2 * count, :].astype(jnp.float32)
    send_ref[:count, :] = far.astype(jnp.bfloat16)
    gain = gain_ref[...] + joined_row(got_ref[2 * count :, :])
    gain_out[...] = gain
    send_ref[count:, :] = split_rows(gain)


def finish_body(at_ref, own_ref, got_ref, gain_in, x_ref, inverse_ref, scale_ref, res_ref, out_ref, gain_out):
    count = own_ref.shape[0]
    rows = pl.multiple_of(at_ref[0] * count, TILE)
    inverse = inverse_ref[pl.ds(rows, count), :]
    normalized = x_ref[pl.ds(rows, count), :].astype(jnp.float32) * inverse
    dnormed = own_ref[...] + got_ref[:count, :].astype(jnp.float32)
    grad_hat = dnormed * scale_ref[...][None, :]
    projection = jnp.mean(grad_hat * normalized, axis=-1, keepdims=True)
    out_ref[...] = (
        res_ref[...].astype(jnp.float32) + inverse * (grad_hat - normalized * projection)
    ).astype(jnp.bfloat16)
    gain_out[...] = (gain_in[...] + joined_row(got_ref[count:, :]))[0]


def add_body(a_ref, b_ref, out_ref):
    out_ref[...] = a_ref[...] + b_ref[...]


def weight_body(at_ref, dp_ref, *refs, offsets, chunks, ranks, stride, last):
    refs = list(refs)
    if ranks:
        parts = [refs.pop(0) for _ in range(ranks)]
    else:
        owned_ref, before_ref, bias_before_ref = refs.pop(0), refs.pop(0), refs.pop(0)
    blocks = [[refs.pop(0) for _ in offsets[c]] for c in range(chunks)]
    out_ref, bias_ref = refs.pop(0), refs.pop(0)
    if ranks:
        owned_ref = refs.pop(0)
        for near, ref in enumerate(parts):
            for far in range(2):
                span = ref.shape[3]
                rows = pl.multiple_of((at_ref[0] ^ (near + 2 * far)) * stride, TILE)
                for high in range(2):
                    count = ref.shape[2]
                    owned_ref[high * count : (high + 1) * count, pl.ds(rows, span), :] = ref[far, high]
    if last:
        stage_ref, sems = refs
        copies = []
    size = owned_ref.shape[0]

    def source(k):
        ring_at = jnp.where(dp_ref[0] % 2 == 0, dp_ref[0] // 2, size - 1 - dp_ref[0] // 2)
        behind = (ring_at + size - k) % size
        return jnp.where(behind < size // 2, 2 * behind, 2 * (size - 1 - behind) + 1) ^ dp_ref[0]

    start = 0
    for c in range(chunks):
        groups = [list(range(i, min(i + 2, len(offsets[c])))) for i in range(0, len(offsets[c]), 2)]
        lefts = [jnp.concatenate([owned_ref[source(offsets[c][i])] for i in group], 1) for group in groups]
        cols = blocks[c][0].shape[1]
        for inner in range(0, cols, 2 * BLOCK):
            here = slice(start + inner, start + inner + 2 * BLOCK)
            total = None if ranks else before_ref[:, here]
            bias = None if ranks else bias_before_ref[here]
            for left, group in zip(lefts, groups):
                right = jnp.concatenate([blocks[c][i][:, inner : inner + 2 * BLOCK] for i in group], 0)
                part = jnp.dot(left, right, preferred_element_type=jnp.float32)
                total = part if total is None else total + part
                row = jnp.sum(right.astype(jnp.float32), axis=0)
                bias = row if bias is None else bias + row
            bias_ref[here] = bias
            if last:
                stage_ref[:, here] = total
                copy = pltpu.make_async_copy(
                    stage_ref.at[:, here], out_ref.at[:, here], sems.at[len(copies)]
                )
                copy.start()
                copies.append(copy)
            else:
                out_ref[:, here] = total
        start += cols
    if last:
        for copy in copies:
            copy.wait()


def snake(size):
    half = size // 2
    return [2 * i for i in range(half)] + [2 * i + 1 for i in reversed(range(half))]


def tiled(dp_size, tensor_size, tokens, width, hidden):
    if dp_size not in (4, 8) or tensor_size != 4:
        return None
    if tokens != LANES or width % (5 * LANES) or width % dp_size or (tokens // tensor_size) % TILE:
        return None
    if hidden % (CHUNKS * BLOCK):
        return None
    owner_rows = width // dp_size
    span = -(-owner_rows // (tensor_size * TILE)) * TILE
    if owner_rows % TILE or (owner_rows - span) % (tensor_size - 1):
        return None
    stride = (owner_rows - span) // (tensor_size - 1)
    if stride % TILE or stride > span or stride <= 0:
        return None
    return stride, span


def on_device(inputs, norm_gain, fc1_weight, fc1_bias, grad_act, grad_res):
    dp_size = lax.axis_size("dp")
    tensor_size = lax.axis_size("tensor")
    tokens, width = inputs.shape
    hidden = fc1_weight.shape[1]
    pieces = tiled(dp_size, tensor_size, tokens, width, hidden)
    if pieces is None:
        return plain(inputs, norm_gain, fc1_weight, fc1_bias, grad_act, grad_res)
    stride, span = pieces
    owner_rows = width // dp_size
    row_count = tokens // tensor_size
    cols = hidden // CHUNKS
    steps = cols // BLOCK
    bf16, f32 = jnp.bfloat16, jnp.float32
    shape = jax.ShapeDtypeStruct

    half = dp_size // 2
    at = lax.axis_index("tensor").astype(jnp.int32).reshape(1)
    dp_at = lax.axis_index("dp").astype(jnp.int32).reshape(1)

    def near(dims, dtype):
        return pltpu.VMEM(dims, dtype)

    def far(array):
        return pltpu.with_memory_space_constraint(array, pltpu.HBM)

    def kernel(name, body, in_specs, out_shape, operands, scratch_shapes=(), out_specs=None):
        with jax.named_scope(name):
            return pl.pallas_call(
                body,
                name=name,
                compiler_params=GRANT,
                in_specs=in_specs,
                out_specs=out_specs or [NEAR] * len(out_shape),
                out_shape=out_shape,
                scratch_shapes=scratch_shapes,
            )(*operands)

    def move(name, array, axis, pairs):
        with jax.named_scope(name):
            return lax.ppermute(array, axis, pairs)

    def swap(name, array, axis, step):
        return move(name, array, axis, [(i, i ^ step) for i in range(lax.axis_size(axis))])

    far_weight = far(fc1_weight)
    sems = pltpu.SemaphoreType.DMA((cols // BLOCK + 4,))
    pre, kept, normed, inverse, x_near, bias_near, act_near = kernel(
        "forward_0",
        functools.partial(forward_body, first=True, chunk=0, cols=cols, stride=stride),
        [SCALAR, SCALAR] + [FAR] * 5,
        [
            near((tokens, cols), bf16),
            near((width, cols), bf16),
            near((tokens, width), bf16),
            near((tokens, 1), f32),
            near((tokens, width), bf16),
            near((hidden,), f32),
            near((tokens, hidden), bf16),
        ],
        (at, dp_at, far(inputs), far(norm_gain), far(fc1_bias), far(grad_act), far_weight),
        [near((width,), f32), sems],
    )
    grad_pre = [pre]
    kept_weight = [kept]
    for c in range(1, CHUNKS):
        pre, kept, stay, send = kernel(
            f"forward_{c}",
            functools.partial(forward_body, first=False, chunk=c, cols=cols, stride=stride),
            [SCALAR, SCALAR, NEAR, NEAR, NEAR, FAR],
            [near((tokens, cols), bf16), near((width, cols), bf16)] + [near((half, span, tokens), bf16)] * 2,
            (at, dp_at, normed, bias_near, act_near, far_weight),
            [near((width, tokens), bf16), sems],
        )
        grad_pre.append(pre)
        kept_weight.append(kept)

    ring = snake(dp_size)
    onward = [(ring[i], ring[(i + 1) % dp_size]) for i in range(dp_size)]
    backward = [(b, a) for a, b in onward]
    found = [{0: piece} for piece in grad_pre]
    for hop in range(1, half + 1):
        for c in range(CHUNKS):
            if hop < half or c % 2 == 0:
                found[c][hop] = move(f"on_{c}_{hop}", found[c][hop - 1], "dp", onward)
            if hop < half or c % 2 == 1:
                found[c][dp_size - hop] = move(
                    f"back_{c}_{hop}", found[c][(dp_size - hop + 1) % dp_size], "dp", backward
                )

    got = swap("owned_0", send, "dp", 1)
    bit = 1
    while 2**bit < dp_size:
        stay, send = kernel(
            f"halve_{bit}",
            functools.partial(halve_body, bit=bit, count=dp_size),
            [SCALAR, NEAR, NEAR],
            [near((half, span, tokens), bf16)] * 2,
            (dp_at, stay, got),
        )
        got = swap(f"owned_{bit}", send, "dp", 2**bit)
        bit += 1
    (piece,) = kernel(
        "join_0", join_body, [NEAR] * 2, [near((2, half, span, tokens), bf16)], (stay, got)
    )
    other = swap("owned_far", piece, "tensor", 2)
    (piece,) = kernel(
        "join_1", join_body, [NEAR] * 2, [near((2, 2, half, span, tokens), bf16)], (piece, other)
    )
    parts = [piece, swap("owned_near", piece, "tensor", 1)]

    stay, send, gain = kernel(
        "backward",
        functools.partial(backward_body, chunks=CHUNKS, feature=5 * LANES),
        [SCALAR] + [NEAR] * (2 * CHUNKS + 2),
        [
            near((2 * row_count, width), bf16),
            near((2 * row_count + TILE, width), bf16),
            near((1, width), f32),
        ],
        (at, *grad_pre, *kept_weight, x_near, inverse),
        [near((tokens, width), bf16)],
    )
    got = swap("term_near", send, "tensor", 1)
    own, send, gain = kernel(
        "merge",
        merge_body,
        [NEAR] * 3,
        [near((row_count, width), f32), near((row_count + TILE, width), bf16), near((1, width), f32)],
        (stay, got, gain),
    )
    got = swap("term_far", send, "tensor", 2)
    grad_inputs, gain = kernel(
        "finish",
        finish_body,
        [SCALAR] + [NEAR] * 7,
        [shape((row_count, width), bf16), shape((width,), f32)],
        (at, own, got, gain, x_near, inverse, norm_gain, grad_res),
    )
    bit = 0
    while 2**bit < dp_size:
        other = swap(f"gain_{bit}", gain, "dp", 2**bit)
        (gain,) = kernel(f"add_{bit}", add_body, [NEAR] * 2, [shape((width,), f32)], (gain, other))
        bit += 1

    def weight_call(name, offsets, carried, last=False):
        opening = carried is None
        operands = parts if opening else list(carried)
        operands = operands + [found[c][k] for c in range(CHUNKS) for k in offsets[c]]
        out_specs = [FAR if last else NEAR, NEAR]
        scratch_shapes = []
        if last:
            out_shape = [shape((owner_rows, hidden), f32), shape((hidden,), f32)]
            scratch_shapes = [pltpu.VMEM((owner_rows, hidden), f32), pltpu.SemaphoreType.DMA((hidden // BLOCK // 2,))]
        else:
            out_shape = [near((owner_rows, hidden), f32), near((hidden,), f32)]
        if opening:
            out_specs.append(NEAR)
            out_shape.append(near((dp_size, owner_rows, tokens), bf16))
        return kernel(
            name,
            functools.partial(
                weight_body,
                offsets=offsets,
                chunks=CHUNKS,
                ranks=2 if opening else 0,
                stride=stride,
                last=last,
            ),
            [SCALAR] * 2 + [NEAR] * len(operands),
            out_shape,
            (at, dp_at, *operands),
            scratch_shapes,
            out_specs,
        )

    close = [0, 1, dp_size - 1]
    wide = [k for k in range(dp_size) if k not in close and k != half]
    total, bias, owned = weight_call("weight_near", [close] * CHUNKS, None)
    if wide:
        total, bias = weight_call("weight_far", [wide] * CHUNKS, (owned, total, bias))
    grad_weight, grad_bias = weight_call("weight_last", [[half]] * CHUNKS, (owned, total, bias), last=True)
    return (grad_inputs, grad_weight, grad_bias, gain)


def solution(mesh):
    in_specs = (
        P("dp", None),
        P(),
        P(None, "tensor"),
        P("tensor"),
        P("dp", "tensor"),
        P(("dp", "tensor"), None),
    )
    out_specs = (P(("dp", "tensor"), None), P("dp", "tensor"), P("tensor"), P())
    return jax.shard_map(
        on_device, mesh=mesh, in_specs=in_specs, out_specs=out_specs, check_vma=False
    )
```

```python
import functools

import jax
import jax.numpy as jnp
from jax import lax
from jax.experimental import pallas as pl
from jax.experimental.pallas import tpu as pltpu
from jax.sharding import PartitionSpec as P


epsilon = 1e-06
CHUNKS = 2
AHEAD = 1
BLOCK = 256
TILE = 16
LANES = 128

VMEM_GRANT = 12 * 1024 * 1024


def gelu_slope(preact):
    return (
        0.5 * (1.0 + lax.erf(preact * 0.7071067811865476))
        + preact * jnp.exp(-0.5 * preact * preact) * 0.3989422804014327
    )


def plain(inputs, norm_gain, fc1_weight, fc1_bias, grad_act, grad_res):
    dp_size = lax.axis_size("dp")
    tensor_size = lax.axis_size("tensor")
    tokens, width = inputs.shape
    owner_rows = width // dp_size
    values = inputs.astype(jnp.float32)
    inverse = lax.rsqrt(jnp.mean(values * values, axis=-1, keepdims=True) + epsilon)
    normalized = values * inverse
    normed = (normalized * norm_gain).astype(jnp.bfloat16)
    blocks = normed.reshape(tokens, dp_size, owner_rows).transpose(1, 0, 2)
    owned_cols = lax.all_to_all(blocks, "dp", 0, 0, tiled=True).reshape(dp_size * tokens, owner_rows)
    preact = jnp.dot(normed, fc1_weight, preferred_element_type=jnp.float32) + fc1_bias
    grad_pre = (grad_act.astype(jnp.float32) * gelu_slope(preact)).astype(jnp.bfloat16)
    grad_pre_all = lax.all_gather(grad_pre, "dp", axis=0, tiled=True)
    back_term = lax.dot_general(
        grad_pre, fc1_weight, (((1,), (1,)), ((), ())), preferred_element_type=jnp.float32
    )
    dnormed = lax.psum_scatter(
        back_term.astype(jnp.bfloat16), "tensor", scatter_dimension=0, tiled=True
    ).astype(jnp.float32)
    grad_weight = lax.dot_general(
        owned_cols, grad_pre_all, (((0,), (0,)), ((), ())), preferred_element_type=jnp.float32
    )
    grad_bias = jnp.sum(grad_pre_all.astype(jnp.float32), axis=0)
    row_count = tokens // tensor_size
    row_start = lax.axis_index("tensor") * row_count
    normalized_rows = lax.dynamic_slice_in_dim(normalized, row_start, row_count, 0)
    inverse_rows = lax.dynamic_slice_in_dim(inverse, row_start, row_count, 0)
    gain_part = jnp.sum(dnormed * normalized_rows, axis=0)
    grad_hat = dnormed * norm_gain
    projection = jnp.mean(grad_hat * normalized_rows, axis=-1, keepdims=True)
    grad_inputs = (
        grad_res.astype(jnp.float32) + inverse_rows * (grad_hat - normalized_rows * projection)
    ).astype(jnp.bfloat16)
    grad_gain = lax.psum(gain_part, ("dp", "tensor"))
    return (grad_inputs, grad_weight, grad_bias, grad_gain)


SCALAR = pl.BlockSpec(memory_space=pltpu.SMEM)
GRANT = pltpu.CompilerParams(vmem_limit_bytes=VMEM_GRANT)
NEAR = pl.BlockSpec(memory_space=pltpu.VMEM)
FAR = pl.BlockSpec(memory_space=pltpu.HBM)


def forward_body(*refs, first, chunk, cols, stride, ahead):
    refs = list(refs)
    at_ref, dp_ref = refs.pop(0), refs.pop(0)
    if first:
        x_far, gain_far, bias_far, act_far, w_ref = (refs.pop(0) for _ in range(5))
        pre_ref, kept_ref, next_ref, normed_ref, inverse_ref, x_ref, bias_ref, act_ref = (refs.pop(0) for _ in range(8))
        gain_ref = refs.pop(0)
    else:
        normed_ref, bias_ref, act_ref, part_ref, w_ref = (refs.pop(0) for _ in range(5))
        pre_ref, kept_ref, stay_ref, send_ref, turned_ref = (refs.pop(0) for _ in range(5))
    sems = refs.pop(0)
    blocks = cols // BLOCK
    skip = 0 if first else ahead

    def fetch(of_chunk, i, target, at, sem):
        return pltpu.make_async_copy(
            w_ref.at[:, pl.ds(of_chunk * cols + i * BLOCK, BLOCK)], target.at[:, pl.ds(at * BLOCK, BLOCK)], sems.at[sem]
        )

    extra = []
    if first:
        pairs = [(x_far, x_ref), (gain_far, gain_ref), (act_far, act_ref), (bias_far, bias_ref)]
        extra = [pltpu.make_async_copy(away, here, sems.at[2 * blocks + i]) for i, (away, here) in enumerate(pairs)]
        extra[0].start()
        extra[1].start()
    copies = [fetch(chunk, i, kept_ref, i - skip, i) for i in range(skip, blocks)]
    following = [fetch(chunk + 1, i, next_ref, i, blocks + i) for i in range(ahead)] if first else []
    for copy in copies + extra[2:]:
        copy.start()
    if first:
        extra[0].wait()
        extra[1].wait()
        values = x_ref[...].astype(jnp.float32)
        inverse = lax.rsqrt(jnp.mean(values * values, axis=-1, keepdims=True) + epsilon)
        normed_ref[...] = (values * inverse * gain_ref[...][None, :]).astype(jnp.bfloat16)
        inverse_ref[...] = inverse
        for copy in copies + extra[2:]:
            copy.wait()
        for copy in following:
            copy.start()
    else:
        kept_owners, span, _ = send_ref.shape
        width = normed_ref.shape[1]
        for i in range(width // LANES):
            turned_ref[i * LANES : (i + 1) * LANES, :] = normed_ref[:, i * LANES : (i + 1) * LANES].T
        low = dp_ref[0] % 2
        for half_owner in range(kept_owners):
            for target, bit in ((stay_ref, low), (send_ref, 1 - low)):
                owner = 2 * half_owner + bit
                start = pl.multiple_of(owner * (width // (2 * kept_owners)) + at_ref[0] * stride, TILE)
                target[half_owner] = turned_ref[pl.ds(start, span), :]

    def close(i, preact):
        here = slice(i * BLOCK, (i + 1) * BLOCK)
        there = slice(chunk * cols + i * BLOCK, chunk * cols + (i + 1) * BLOCK)
        slope = gelu_slope(preact + bias_ref[there][None, :])
        pre_ref[:, here] = (act_ref[:, there].astype(jnp.float32) * slope).astype(jnp.bfloat16)

    held = None
    for i in range(blocks):
        if i < skip:
            right = part_ref[:, i * BLOCK : (i + 1) * BLOCK]
        else:
            if not first and i == skip:
                for copy in copies:
                    copy.wait()
            right = kept_ref[:, (i - skip) * BLOCK : (i - skip + 1) * BLOCK]
        preact = jnp.dot(normed_ref[...], right, preferred_element_type=jnp.float32)
        if held is not None:
            close(i - 1, held)
        held = preact
    close(blocks - 1, held)
    for copy in following:
        copy.wait()


def cut_body(on_ref, back_ref, on_out, back_out):
    cols = on_out.shape[1]
    on_out[...] = on_ref[:, :cols]
    back_out[...] = back_ref[:, cols:]


def spread_body(dp_ref, stay_ref, got_ref, gain_ref, *outs):
    span = stay_ref.shape[1]
    gain = gain_ref[...]
    for away, out in enumerate(outs):
        owner = (dp_ref[0] // 2) ^ away
        out[:span] = stay_ref[owner]
        out[span : 2 * span] = got_ref[owner]
        out[2 * span :] = gain.astype(jnp.bfloat16)


def join_body(*refs):
    pieces, gain_ref, out, gain_out = refs[:-3], refs[-3], refs[-2], refs[-1]
    count = gain_ref.shape[0]
    gain = gain_ref[...]
    rows = pieces[0].shape[0] - count
    for i, ref in enumerate(pieces):
        out[i * rows : (i + 1) * rows] = ref[:rows]
        if i:
            gain = gain + ref[rows:].astype(jnp.float32)
    gain_out[...] = gain
    out[len(pieces) * rows :] = gain.astype(jnp.bfloat16)


def backward_body(at_ref, *refs, chunks, kept, feature):
    pre_refs = refs[:chunks]
    kept_refs = refs[chunks : chunks + kept]
    x_ref, inverse_ref, stay_ref, send_ref, gain_ref, term_ref = refs[chunks + kept :]
    count = stay_ref.shape[0] // 2
    cols = pre_refs[0].shape[1]
    for j in range(x_ref.shape[1] // feature):
        here = slice(j * feature, (j + 1) * feature)
        term = None
        start = 0
        for kept_ref in kept_refs:
            size = kept_ref.shape[1]
            left = pre_refs[start // cols][:, start % cols : start % cols + size]
            part = lax.dot_general(
                left, kept_ref[here, :], (((1,), (1,)), ((), ())), preferred_element_type=jnp.float32
            )
            term = part if term is None else term + part
            start += size
        term = term.astype(jnp.bfloat16)
        term_ref[:, here] = term
        normalized = x_ref[:, here].astype(jnp.float32) * inverse_ref[...]
        gain = jnp.sum(term.astype(jnp.float32) * normalized, axis=0, keepdims=True)
        for i in range(feature // LANES):
            row = j * (feature // LANES) + i
            gain_ref[row : row + 1, :] = gain[:, i * LANES : (i + 1) * LANES]
    used = x_ref.shape[1] // LANES
    gain_ref[used:, :] = jnp.zeros((gain_ref.shape[0] - used, LANES), jnp.float32)
    for slot in range(2):
        for ref, flip in ((stay_ref, 0), (send_ref, 1)):
            rows = pl.multiple_of((at_ref[0] ^ (flip + 2 * slot)) * count, TILE)
            ref[slot * count : (slot + 1) * count, :] = term_ref[pl.ds(rows, count), :]


def merge_body(stay_ref, got_ref, own_ref, send_ref):
    count = own_ref.shape[0]
    own_ref[...] = stay_ref[:count, :].astype(jnp.float32) + got_ref[:count, :].astype(jnp.float32)
    away = stay_ref[count:, :].astype(jnp.float32) + got_ref[count:, :].astype(jnp.float32)
    send_ref[...] = away.astype(jnp.bfloat16)


def finish_body(at_ref, own_ref, got_ref, x_ref, inverse_ref, scale_ref, res_ref, out_ref):
    count = own_ref.shape[0]
    rows = pl.multiple_of(at_ref[0] * count, TILE)
    inverse = inverse_ref[pl.ds(rows, count), :]
    normalized = x_ref[pl.ds(rows, count), :].astype(jnp.float32) * inverse
    dnormed = own_ref[...] + got_ref[...].astype(jnp.float32)
    grad_hat = dnormed * scale_ref[...][None, :]
    projection = jnp.mean(grad_hat * normalized, axis=-1, keepdims=True)
    out_ref[...] = (
        res_ref[...].astype(jnp.float32) + inverse * (grad_hat - normalized * projection)
    ).astype(jnp.bfloat16)


def block_source(dp_ref, size, k):
    ring_at = jnp.where(dp_ref[0] % 2 == 0, dp_ref[0] // 2, size - 1 - dp_ref[0] // 2)
    before = (ring_at + size - k) % size
    return jnp.where(before < size // 2, 2 * before, 2 * (size - 1 - before) + 1) ^ dp_ref[0]


def weight_body(at_ref, dp_ref, *refs, offsets, chunks, opening, stride):
    refs = list(refs)
    if opening:
        parts = [refs.pop(0), refs.pop(0)]
        gain_in = refs.pop(0)
    else:
        owned_ref, before_ref, bias_before_ref = refs.pop(0), refs.pop(0), refs.pop(0)
    blocks = [[refs.pop(0) for _ in offsets] for _ in range(chunks)]
    out_ref, bias_ref = refs.pop(0), refs.pop(0)
    if opening:
        owned_ref, gain_ref = refs.pop(0), refs.pop(0)
        owners = owned_ref.shape[0]
        count = gain_in.shape[0]
        span = (parts[0].shape[0] - count) // (2 * owners)
        for close, ref in enumerate(parts):
            for away in range(2):
                rows = pl.multiple_of((at_ref[0] ^ (close + 2 * away)) * stride, TILE)
                for owner in range(owners):
                    start = (away * owners + owner) * span
                    owned_ref[owner, pl.ds(rows, span), :] = ref[start : start + span]
        gain = gain_in[...] + parts[1][2 * owners * span :].astype(jnp.float32)
        gain_ref[...] = gain
    groups = [list(range(i, min(i + 2, len(offsets)))) for i in range(0, len(offsets), 2)]
    size = owned_ref.shape[0]
    lefts = [
        jnp.concatenate([owned_ref[block_source(dp_ref, size, offsets[i])] for i in group], 1) for group in groups
    ]
    start = 0
    for c in range(chunks):
        cols = blocks[c][0].shape[1]
        for inner in range(0, cols, 2 * BLOCK):
            here = slice(start + inner, start + inner + 2 * BLOCK)
            total = None if opening else before_ref[:, here]
            bias = None if opening else bias_before_ref[here]
            for left, group in zip(lefts, groups):
                right = jnp.concatenate([blocks[c][i][:, inner : inner + 2 * BLOCK] for i in group], 0)
                part = jnp.dot(left, right, preferred_element_type=jnp.float32)
                total = part if total is None else total + part
                row = jnp.sum(right.astype(jnp.float32), axis=0)
                bias = row if bias is None else bias + row
            bias_ref[here] = bias
            out_ref[:, here] = total
        start += cols


def weight_last_body(dp_ref, *refs, offset, chunk, cols):
    refs = list(refs)
    if chunk:
        refs.pop(0)
        gain_a, gain_b, gain_ref = refs.pop(0), refs.pop(0), refs.pop(7)
    owned_ref, before_ref, bias_before_ref, left_ref, right_ref, out_ref, bias_ref, stage_ref, sems = refs
    left = owned_ref[block_source(dp_ref, owned_ref.shape[0], offset)]
    bias_ref[...] = bias_before_ref[...]
    copies = []
    for i in range(cols // BLOCK):
        here = slice(i * BLOCK, (i + 1) * BLOCK)
        there = slice(chunk * cols + i * BLOCK, chunk * cols + (i + 1) * BLOCK)
        ref, start = (left_ref, i * BLOCK) if i * BLOCK < cols // 2 else (right_ref, i * BLOCK - cols // 2)
        right = ref[:, start : start + BLOCK]
        stage_ref[:, here] = before_ref[:, there] + jnp.dot(left, right, preferred_element_type=jnp.float32)
        copy = pltpu.make_async_copy(stage_ref.at[:, here], out_ref.at[:, there], sems.at[i])
        copy.start()
        copies.append(copy)
        bias_ref[there] = bias_before_ref[there] + jnp.sum(right.astype(jnp.float32), axis=0)
    if chunk:
        gain = gain_a[...] + gain_b[...]
        for i in range(gain_ref.shape[0] // LANES):
            gain_ref[i * LANES : (i + 1) * LANES] = gain[i]
    for copy in copies:
        copy.wait()


def snake(size):
    half = size // 2
    return [2 * i for i in range(half)] + [2 * i + 1 for i in reversed(range(half))]


def tiled(dp_size, tensor_size, tokens, width, hidden):
    if dp_size != 8 or tensor_size != 4:
        return None
    if tokens != LANES or width % (5 * LANES) or width % dp_size or (tokens // tensor_size) % TILE:
        return None
    if hidden % (CHUNKS * BLOCK):
        return None
    owner_rows = width // dp_size
    span = -(-owner_rows // (tensor_size * TILE)) * TILE
    if owner_rows % TILE or (owner_rows - span) % (tensor_size - 1):
        return None
    stride = (owner_rows - span) // (tensor_size - 1)
    if stride % TILE or stride > span or stride <= 0:
        return None
    return stride, span


def on_device(inputs, norm_gain, fc1_weight, fc1_bias, grad_act, grad_res):
    dp_size = lax.axis_size("dp")
    tensor_size = lax.axis_size("tensor")
    tokens, width = inputs.shape
    hidden = fc1_weight.shape[1]
    pieces = tiled(dp_size, tensor_size, tokens, width, hidden)
    if pieces is None:
        return plain(inputs, norm_gain, fc1_weight, fc1_bias, grad_act, grad_res)
    stride, span = pieces
    owner_rows = width // dp_size
    row_count = tokens // tensor_size
    cols = hidden // CHUNKS
    bf16, f32 = jnp.bfloat16, jnp.float32
    shape = jax.ShapeDtypeStruct

    half = dp_size // 2
    at = lax.axis_index("tensor").astype(jnp.int32).reshape(1)
    dp_at = lax.axis_index("dp").astype(jnp.int32).reshape(1)

    def near(dims, dtype):
        return pltpu.VMEM(dims, dtype)

    def far(array):
        return pltpu.with_memory_space_constraint(array, pltpu.HBM)

    def kernel(body, in_specs, out_shape, operands, scratch_shapes=(), out_specs=None, aliases=None):
        return pl.pallas_call(
            body,
            compiler_params=GRANT,
            in_specs=in_specs,
            out_specs=out_specs or [NEAR] * len(out_shape),
            out_shape=out_shape,
            scratch_shapes=scratch_shapes,
            input_output_aliases=aliases or {},
        )(*operands)

    def swap(array, axis, step):
        return lax.ppermute(array, axis, [(i, i ^ step) for i in range(lax.axis_size(axis))])

    far_weight = far(fc1_weight)
    blocks = cols // BLOCK
    sems = pltpu.SemaphoreType.DMA((2 * blocks + 4,))
    pre, kept, part, normed, inverse, x_near, bias_near, act_near = kernel(
        functools.partial(forward_body, first=True, chunk=0, cols=cols, stride=stride, ahead=AHEAD),
        [SCALAR, SCALAR] + [FAR] * 5,
        [
            near((tokens, cols), bf16),
            near((width, cols), bf16),
            near((width, AHEAD * BLOCK), bf16),
            near((tokens, width), bf16),
            near((tokens, 1), f32),
            near((tokens, width), bf16),
            near((hidden,), f32),
            near((tokens, hidden), bf16),
        ],
        (at, dp_at, far(inputs), far(norm_gain), far(fc1_bias), far(grad_act), far_weight),
        [near((width,), f32), sems],
    )
    pre_1, rest, stay, send = kernel(
        functools.partial(forward_body, first=False, chunk=1, cols=cols, stride=stride, ahead=AHEAD),
        [SCALAR, SCALAR, NEAR, NEAR, NEAR, NEAR, FAR],
        [near((tokens, cols), bf16), near((width, cols - AHEAD * BLOCK), bf16)]
        + [near((half, span, tokens), bf16)] * 2,
        (at, dp_at, normed, bias_near, act_near, part, far_weight),
        [near((width, tokens), bf16), sems],
    )
    grad_pre = [pre, pre_1]
    kept_weight = [kept, part, rest]

    ring = snake(dp_size)
    onward = [(ring[i], ring[(i + 1) % dp_size]) for i in range(dp_size)]
    backward = [(b, a) for a, b in onward]
    found = [{0: piece} for piece in grad_pre]
    for hop in range(1, half):
        for c in range(CHUNKS):
            found[c][hop] = lax.ppermute(found[c][hop - 1], "dp", onward)
            found[c][dp_size - hop] = lax.ppermute(found[c][(dp_size - hop + 1) % dp_size], "dp", backward)
    ends = []
    for c in range(CHUNKS):
        left, right = kernel(
            cut_body, [NEAR] * 2, [near((tokens, cols // 2), bf16)] * 2, (found[c][half - 1], found[c][half + 1])
        )
        ends.append([lax.ppermute(left, "dp", onward), lax.ppermute(right, "dp", backward)])

    gain_rows = -(-width // (LANES * TILE)) * TILE
    term_stay, term_send, gain = kernel(
        functools.partial(backward_body, chunks=CHUNKS, kept=len(kept_weight), feature=5 * LANES),
        [SCALAR] + [NEAR] * (CHUNKS + len(kept_weight) + 2),
        [near((2 * row_count, width), bf16)] * 2
        + [near((gain_rows, tokens), f32)],
        (at, *grad_pre, *kept_weight, x_near, inverse),
        [near((tokens, width), bf16)],
    )
    got = swap(send, "dp", 1)
    pieces = kernel(
        spread_body,
        [SCALAR] + [NEAR] * 3,
        [near((2 * span + gain_rows, tokens), bf16)] * half,
        (dp_at, stay, got, gain),
    )
    pieces = [pieces[0]] + [swap(pieces[away], "dp", 2 * away) for away in range(1, half)]
    for count, step in ((1, 2), (2, 1)):
        piece, gain = kernel(
            join_body,
            [NEAR] * (len(pieces) + 1),
            [near((count * dp_size * span + gain_rows, tokens), bf16), near((gain_rows, tokens), f32)],
            (*pieces, gain),
        )
        pieces = [piece, swap(piece, "tensor", step)]
    parts = [*pieces, gain]

    got = swap(term_send, "tensor", 1)
    own, term_send = kernel(
        merge_body, [NEAR] * 2, [near((row_count, width), f32), near((row_count, width), bf16)], (term_stay, got)
    )
    got = swap(term_send, "tensor", 2)
    (grad_inputs,) = kernel(
        finish_body,
        [SCALAR] + [NEAR] * 6,
        [shape((row_count, width), bf16)],
        (at, own, got, x_near, inverse, norm_gain, grad_res),
    )

    def weight_call(offsets, carried):
        opening = carried is None
        operands = parts if opening else list(carried)
        operands = operands + [found[c][k] for c in range(CHUNKS) for k in offsets]
        out_shape = [near((owner_rows, hidden), f32), near((hidden,), f32)]
        if opening:
            out_shape += [near((dp_size, owner_rows, tokens), bf16), near((gain_rows, tokens), f32)]
        return kernel(
            functools.partial(weight_body, offsets=offsets, chunks=CHUNKS, opening=opening, stride=stride),
            [SCALAR] * 2 + [NEAR] * len(operands),
            out_shape,
            (at, dp_at, *operands),
        )

    close = [0, 1, dp_size - 1]
    wide = [k for k in range(dp_size) if k not in close and k != half]
    total, bias, owned, gain = weight_call(close, None)
    gain_got = swap(gain, "dp", 1)
    if wide:
        total, bias = weight_call(wide, (owned, total, bias))
    grad_weight = None
    for c in range(CHUNKS):
        started = [] if c == 0 else [grad_weight]
        gains = [] if c == 0 else [gain, gain_got]
        grad_weight, bias, *grad_gain = kernel(
            functools.partial(weight_last_body, offset=half, chunk=c, cols=cols),
            [SCALAR] + [FAR] * len(started) + [NEAR] * (5 + len(gains)),
            [shape((owner_rows, hidden), f32), shape((hidden,), f32)] + [shape((width,), f32)] * len(started),
            (dp_at, *started, *gains, owned, total, bias, *ends[c]),
            [near((owner_rows, cols), f32), sems],
            [FAR, NEAR] + [NEAR] * len(started),
            {1: 0} if started else {},
        )
    return (grad_inputs, grad_weight, bias, *grad_gain)


def solution(mesh):
    in_specs = (
        P("dp", None),
        P(),
        P(None, "tensor"),
        P("tensor"),
        P("dp", "tensor"),
        P(("dp", "tensor"), None),
    )
    out_specs = (P(("dp", "tensor"), None), P("dp", "tensor"), P("tensor"), P())
    return jax.shard_map(on_device, mesh=mesh, in_specs=in_specs, out_specs=out_specs, check_vma=False)
```
